32 devices in a mesh: dp: 16 (over z, y, x), mp: 2 (over core).
Axes of the slice: x: 2, y: 2, z: 4, core: 2. Of those that a mesh axis runs over, the one named last changes fastest.
Arguments:
- inputs: bfloat16 [16, 1024, 768], P('dp'), may hold values from -6 to 6
- segments: int32 [16, 1024], P('dp'), may hold values from 0 to 28, as said below
- cotangent: bfloat16 [16, 1024, 768], P('dp'), may hold values from -6 to 6
- norm1_gain: float32 [768], replicated, may hold values from 0.5 to 1.5
- norm1_bias: float32 [768], replicated, may hold values from -3 to 3
- qkv_weight: bfloat16 [3, 768, 768], P(None, None, 'mp'), may hold values from -0.21875 to 0.21875
- qv_bias: float32 [2, 768], P(None, 'mp'), may hold values from -3 to 3
- proj_weight: bfloat16 [768, 768], P('mp'), may hold values from -1.75 to 1.75
- proj_bias: float32 [768], replicated, may hold values from -3 to 3
- norm2_gain: float32 [768], replicated, may hold values from 0.5 to 1.5
- norm2_bias: float32 [768], replicated, may hold values from -3 to 3
- fc1_weight: bfloat16 [768, 3072], P(None, 'mp'), may hold values from -0.21875 to 0.21875
- fc1_bias: float32 [3072], P('mp'), may hold values from -3 to 3
- fc2_weight: bfloat16 [3072, 768], P('mp'), may hold values from -0.109375 to 0.109375
- fc2_bias: float32 [768], replicated, may hold values from -3 to 3
Outputs:
- output: bfloat16 [16, 1024, 768], P('dp')
- input_grad: bfloat16 [16, 1024, 768], P('dp')
- norm1_gain_grad: float32 [768], P('dp')
- norm1_bias_grad: float32 [768], P('dp')
- qkv_weight_grad: float32 [3, 768, 768], P(None, 'dp', 'mp')
- qv_bias_grad: float32 [2, 768], P(None, ('mp', 'dp'))
- proj_weight_grad: float32 [768, 768], P('mp', 'dp')
- proj_bias_grad: float32 [768], P('dp')
- norm2_gain_grad: float32 [768], P('dp')
- norm2_bias_grad: float32 [768], P('dp')
- fc1_weight_grad: float32 [768, 3072], P('dp', 'mp')
- fc1_bias_grad: float32 [3072], P(('mp', 'dp'))
- fc2_weight_grad: float32 [3072, 768], P('mp', 'dp')
- fc2_bias_grad: float32 [768], P('dp')
The draws below stay inside these ranges and needn't reach their ends.
Inputs may be any that keep to these rules, and one draw needn't show every extreme that they name: `segments`: each packed row holds whole images from slot 0 onward, numbered 1, 2, 3 and so on in order, each a run of max(1024 * n // 1024, 1) slots for n one of 576, 400, 256, 225, 144, 100, 64, 36 (patch-size classes of a 240-pixel image); the slots after the last image are 0. One packed row holds only images of the smallest class, as many as fit.
All inputs are finite; a program needn't handle non-finite values.
Results may differ from the reference program's by a relative error of at most 0.013.
Values sent between devices are 32-bit elements; how exact they have to be, the bound alone decides.
No kernel may reach another device: no remote copies, remote signals or barrier semaphores. Data moves between devices by JAX's collectives and lax.ppermute only.
A program may use at most 192 MiB of HBM per device.

```python
import jax
import jax.numpy as jnp
from jax import lax

D = 768
HEAD_DIM = 64
FF = 3072
SEQ = 1024
ROWS = 16


def draw_segments(key, part):
    patch_counts = jnp.array([576, 400, 256, 225, 144, 100, 64, 36], jnp.int32)
    class_len = jnp.maximum(patch_counts * SEQ // 1024, 1)
    classes_drawn = jax.random.randint(key, (ROWS, 48), 0, 8)
    chosen_row = jax.random.randint(jax.random.fold_in(key, 7), (), 0, ROWS)
    row_index = jnp.arange(ROWS, dtype=jnp.int32)
    classes_drawn = jnp.where(row_index[:, None] == chosen_row, 7, classes_drawn)
    image_len = jnp.take(class_len, classes_drawn)
    image_end = jnp.cumsum(image_len, axis=1)
    fitted = image_end <= SEQ
    slot_index = jnp.arange(SEQ, dtype=jnp.int32)
    before = jnp.sum(((image_end[:, None, :] <= slot_index[None, :, None]) & fitted[:, None, :]).astype(jnp.int32), axis=2)
    filled = jnp.sum(jnp.where(fitted, image_len, 0), axis=1)
    return jnp.where(slot_index[None, :] < filled[:, None], before + 1, 0).astype(jnp.int32)


def strengthened(drawn, own_key, source, target, shards_of, factor):
    def block_of(dim):
        return (jnp.arange(drawn.shape[dim]) // (drawn.shape[dim] // shards_of)).reshape((-1,) + (1,) * (drawn.ndim - 1 - dim))

    near = jax.random.permutation(own_key, shards_of)[block_of(target)]
    other_side = (block_of(target) + shards_of // 2) % shards_of
    return jnp.where((block_of(source) == near) | (block_of(source) == other_side), factor * drawn, drawn)


def steps_of(stream_key, dims, pieces, low, high):
    loudness = 1.0
    for position, blocks in pieces:
        heights = jax.random.uniform(jax.random.fold_in(jax.random.fold_in(stream_key, 6), position), (blocks,), jnp.float32, low / len(pieces), high / len(pieces))
        loudness = loudness * jnp.repeat(jnp.exp(heights), dims[position] // blocks).reshape((-1,) + (1,) * (len(dims) - 1 - position))
    return loudness


def scatter_about(stream_key, shape, deviation, most, shards=(), kind=jnp.bfloat16):
    gain = steps_of(stream_key, shape, shards, -0.22, 0.18) if shards else 1.0
    values = jax.random.normal(stream_key, shape, jnp.float32) * deviation * gain
    return jnp.minimum(jnp.maximum(values, -most), most).astype(kind)


def bell_draw_with(own_key, shape, scale, reach, shards, heavy, kind=jnp.bfloat16):
    values = scale * jax.random.normal(own_key, shape, jnp.float32)
    if shards:
        values = values * steps_of(own_key, shape, shards, -0.22, 0.18)
    return jnp.clip(strengthened(values, jax.random.fold_in(own_key, 3), *heavy), -reach, reach).astype(kind)


def setup_inputs(seed: int = 0) -> dict:
    key_list = jax.random.split(jax.random.key(seed), 16)
    inputs = bell_draw_with(key_list[0], (ROWS, SEQ, D), 1.0, 6.0, ((0, 16),), (0, 2, 16, 2.0))
    segments = draw_segments(jax.random.fold_in(key_list[15], 71), 0)
    cotangent = scatter_about(key_list[2], (ROWS, SEQ, D), 1.0, 6.0, ((0, 16),))
    norm1_gain = jnp.clip(1.0 + 0.1 * jax.random.normal(key_list[3], (D,), jnp.float32), 0.5, 1.5)
    norm1_bias = scatter_about(key_list[4], (D,), 0.3, 3.0, (), jnp.float32)
    qkv_weight = scatter_about(key_list[5], (3, D, D), D ** -0.5, 0.21875, ((2, 2),))
    qv_bias = scatter_about(key_list[6], (2, D), 0.3, 3.0, ((1, 2),), jnp.float32)
    proj_weight = scatter_about(key_list[7], (D, D), (D // 64) ** -0.5, 1.75, ((0, 2),))
    proj_bias = scatter_about(key_list[8], (D,), 0.3, 3.0, (), jnp.float32)
    norm2_gain = jnp.clip(1.0 + 0.1 * jax.random.normal(key_list[9], (D,), jnp.float32), 0.5, 1.5)
    norm2_bias = scatter_about(key_list[10], (D,), 0.3, 3.0, (), jnp.float32)
    fc1_weight = scatter_about(key_list[11], (D, FF), D ** -0.5, 0.21875, ((1, 2),))
    fc1_bias = scatter_about(key_list[12], (FF,), 0.3, 3.0, ((0, 2),), jnp.float32)
    fc2_weight = scatter_about(key_list[13], (FF, D), FF ** -0.5, 0.109375, ((0, 2),))
    fc2_bias = scatter_about(key_list[14], (D,), 0.3, 3.0, (), jnp.float32)
    return {"inputs": inputs, "segments": segments, "cotangent": cotangent, "norm1_gain": norm1_gain, "norm1_bias": norm1_bias, "qkv_weight": qkv_weight, "qv_bias": qv_bias, "proj_weight": proj_weight, "proj_bias": proj_bias, "norm2_gain": norm2_gain, "norm2_bias": norm2_bias, "fc1_weight": fc1_weight, "fc1_bias": fc1_bias, "fc2_weight": fc2_weight, "fc2_bias": fc2_bias}


EPSILON = 1e-06
NEG_FILL = -1000000000.0
HIGHEST = lax.Precision.HIGHEST

@jax.custom_vjp
def low(v):
    return lax.optimization_barrier(v.astype(jnp.bfloat16)).astype(jnp.float32)

@jax.custom_vjp
def low_back(v):
    return v

def low_keep(v):
    return (low(v), None)

def low_pass(kept, grad):
    return (grad,)

def back_keep(v):
    return (v, None)

def back_low(kept, grad):
    return (low(grad),)
low.defvjp(low_keep, low_pass)
low_back.defvjp(back_keep, back_low)

def layer_norm(values, gain_vec, shift_vec):
    center = values - lax.optimization_barrier(jnp.mean(values, axis=-1, keepdims=True))
    spread = lax.optimization_barrier(jnp.mean(center * center, axis=-1, keepdims=True))
    return center * lax.rsqrt(spread + EPSILON) * gain_vec + shift_vec

def matmul(left_side, right_side):
    return jnp.dot(left_side, right_side, precision=HIGHEST)

def attend_row(operands):
    query_row, key_row, value_row, seg_row = operands
    head_count = query_row.shape[-1] // HEAD_DIM
    query_heads = query_row.reshape(SEQ, head_count, HEAD_DIM)
    key_heads = key_row.reshape(SEQ, head_count, HEAD_DIM)
    value_heads = value_row.reshape(SEQ, head_count, HEAD_DIM)
    scores = jnp.einsum('qhd,khd->hqk', query_heads, key_heads, precision=HIGHEST) * HEAD_DIM ** (-0.5)
    scores = low_back(scores)
    allowed = (seg_row[:, None] == seg_row[None, :]) & (seg_row[:, None] > 0)
    scores = jnp.where(allowed[None], scores, NEG_FILL)
    row_max = lax.optimization_barrier(jnp.max(scores, axis=-1, keepdims=True))
    exponent = jnp.exp(scores - row_max)
    weights = low(exponent / lax.optimization_barrier(jnp.sum(exponent, axis=-1, keepdims=True)))
    mixed_rows = jnp.einsum('hqk,khd->qhd', weights, value_heads, precision=HIGHEST)
    mixed_rows = mixed_rows.reshape(SEQ, head_count * HEAD_DIM)
    return mixed_rows * (seg_row > 0).astype(mixed_rows.dtype)[:, None]

def forward(group_in, seg_group, params):
    norm1_gain, norm1_bias, qkv_weight, qv_bias, proj_weight, proj_bias, norm2_gain, norm2_bias, fc1_weight, fc1_bias, fc2_weight, fc2_bias = params
    rows_here = group_in.shape[0]
    flat_in = group_in.reshape(rows_here * SEQ, D)
    normed1 = low(layer_norm(flat_in, norm1_gain, norm1_bias))
    queries = low(low_back(matmul(normed1, qkv_weight[0]) + qv_bias[0]))
    key_rows = low(low_back(matmul(normed1, qkv_weight[1])))
    value_rows = low(low_back(matmul(normed1, qkv_weight[2]) + qv_bias[1]))
    row_shape = (rows_here, SEQ, D)
    attended = lax.map(jax.checkpoint(attend_row), (queries.reshape(row_shape), key_rows.reshape(row_shape), value_rows.reshape(row_shape), seg_group))
    attended = low(low_back(attended.reshape(rows_here * SEQ, D)))
    branch = low_back(matmul(attended, proj_weight) + proj_bias)
    middle = flat_in + branch
    normed2 = low(layer_norm(middle, norm2_gain, norm2_bias))
    hidden = low_back(matmul(normed2, fc1_weight) + fc1_bias)
    active = low(jax.nn.gelu(hidden, approximate=False))
    result = middle + low_back(matmul(active, fc2_weight) + fc2_bias)
    return result.reshape(row_shape)

def reference(inputs, segments, cotangent, norm1_gain, norm1_bias, qkv_weight, qv_bias, proj_weight, proj_bias, norm2_gain, norm2_bias, fc1_weight, fc1_bias, fc2_weight, fc2_bias):
    params = jax.tree.map(lambda member: member.astype(jnp.float32), (norm1_gain, norm1_bias, qkv_weight, qv_bias, proj_weight, proj_bias, norm2_gain, norm2_bias, fc1_weight, fc1_bias, fc2_weight, fc2_bias))
    group_rows = max(1, min(ROWS, 4096 // SEQ))
    while ROWS % group_rows != 0:
        group_rows = group_rows - 1
    group_total = ROWS // group_rows
    inputs_all = inputs.astype(jnp.float32).reshape(group_total, group_rows, SEQ, D)
    segs_all = segments.reshape(group_total, group_rows, SEQ)
    cots_all = cotangent.astype(jnp.float32).reshape(group_total, group_rows, SEQ, D)
    zero_grads = jax.tree.map(jnp.zeros_like, params)

    def group_step(totals, slab):
        group_in, seg_group, cot_group = slab
        result, pull = jax.vjp(lambda first, second: forward(first, seg_group, second), group_in, params)
        live = (seg_group > 0).astype(jnp.float32)[..., None]
        grad_in, grad_params = pull(cot_group * live)
        totals = jax.tree.map(lambda left_side, right_side: left_side + right_side, totals, grad_params)
        return (totals, (result.astype(jnp.bfloat16), grad_in.astype(jnp.bfloat16)))
    totals, (outs_all, grads_all) = lax.scan(group_step, zero_grads, (inputs_all, segs_all, cots_all))
    return (outs_all.reshape(ROWS, SEQ, D), grads_all.reshape(ROWS, SEQ, D), totals[0], totals[1], totals[2], totals[3], totals[4], totals[5], totals[6], totals[7], totals[8], totals[9], totals[10], totals[11])
```

```python
from functools import partial

import jax
import jax.numpy as jnp
from jax import lax
from jax.sharding import PartitionSpec as P

HEAD_DIM = 64


EPSILON = 1e-06
NEG_FILL = -1000000000.0


def layer_norm(values, gain_vec, shift_vec):
    center = values - jnp.mean(values, axis=-1, keepdims=True)
    inv_spread = lax.rsqrt(jnp.mean(center * center, axis=-1, keepdims=True) + EPSILON)
    normed = center * inv_spread
    return (normed * gain_vec + shift_vec, normed, inv_spread)


def norm_back(grad_out, normed, inv_spread, gain_vec):
    scaled = grad_out * gain_vec
    grad_in = inv_spread * (
        scaled
        - jnp.mean(scaled, axis=-1, keepdims=True)
        - normed * jnp.mean(scaled * normed, axis=-1, keepdims=True)
    )
    return (grad_in, jnp.sum(grad_out * normed, axis=0), jnp.sum(grad_out, axis=0))


def product(left_side, right_side):
    return jnp.dot(left_side, right_side, preferred_element_type=jnp.float32)


def row_contract(left_side, right_side):
    return lax.dot_general(
        left_side, right_side, (((0,), (0,)), ((), ())), preferred_element_type=jnp.float32
    )


def back_product(left_side, right_side):
    return lax.dot_general(
        left_side, right_side, (((1,), (1,)), ((), ())), preferred_element_type=jnp.float32
    )


X_FIRST = (0, 1, 2, 3)
Y_FIRST = (1, 0, 2, 3)
Z_FIRST = (2, 3, 0, 1)


def pair_sum(values):
    if lax.axis_size("mp") != 2:
        return lax.psum(values, "mp")
    return values + lax.ppermute(values, "mp", [(0, 1), (1, 0)])


def blocks_of(grad, block_count):
    return grad.reshape(block_count, grad.shape[0] // block_count, grad.shape[1])


def sum_rows(blocks, order):
    count, rows, columns = blocks.shape
    bits = count.bit_length() - 1
    if count != 1 << bits:
        return lax.psum_scatter(blocks, "dp", scatter_dimension=0, tiled=True)[0]
    me = lax.axis_index("dp")
    order = [bit for bit in order if bit < bits] + list(range(len(order), bits))
    axes = list(range(bits))[::-1]
    held = blocks.reshape((2,) * bits + (rows, columns))
    for bit in order:
        axis = axes.index(bit)
        mine = (me >> bit) & 1
        kept = lax.dynamic_index_in_dim(held, mine, axis, keepdims=False)
        sent = lax.dynamic_index_in_dim(held, 1 - mine, axis, keepdims=False)
        held = kept + lax.ppermute(sent, "dp", [(i, i ^ (1 << bit)) for i in range(count)])
        axes.pop(axis)
    return held


def block_scores(query_block, key_heads, seg_block, seg_row, score_scale):
    scores = (
        jnp.einsum("qhd,khd->hqk", query_block, key_heads, preferred_element_type=jnp.float32)
        * score_scale
    )
    allowed = (seg_block[:, None] == seg_row[None, :]) & (seg_block[:, None] > 0)
    return jnp.where(allowed[None], scores, NEG_FILL)


def row_forward(operands):
    query_row, key_row, value_row, seg_row = operands
    seq_len = query_row.shape[0]
    head_count = query_row.shape[1] // HEAD_DIM
    block_len = min(512, seq_len)
    score_scale = HEAD_DIM ** (-0.5)
    query_heads = query_row.reshape(seq_len, head_count, HEAD_DIM)
    key_heads = key_row.reshape(seq_len, head_count, HEAD_DIM)
    value_heads = value_row.reshape(seq_len, head_count, HEAD_DIM)
    outputs = []
    log_parts = []
    for offset in range(0, seq_len, block_len):
        scores = block_scores(
            query_heads[offset : offset + block_len],
            key_heads,
            seg_row[offset : offset + block_len],
            seg_row,
            score_scale,
        )
        row_max = jnp.max(scores, axis=-1, keepdims=True)
        exponent = jnp.exp(scores - row_max)
        row_total = jnp.sum(exponent, axis=-1, keepdims=True)
        weights = (exponent / row_total).astype(jnp.bfloat16)
        mixed_rows = jnp.einsum(
            "hqk,khd->qhd", weights, value_heads, preferred_element_type=jnp.float32
        )
        outputs.append(mixed_rows.reshape(block_len, head_count * HEAD_DIM))
        log_parts.append((row_max + jnp.log(row_total))[..., 0])
    return (jnp.concatenate(outputs, axis=0), jnp.concatenate(log_parts, axis=1))


def row_backward(operands):
    query_row, key_row, value_row, seg_row, grad_row, log_total = operands
    seq_len = query_row.shape[0]
    head_count = query_row.shape[1] // HEAD_DIM
    block_len = min(512, seq_len)
    score_scale = HEAD_DIM ** (-0.5)
    query_heads = query_row.reshape(seq_len, head_count, HEAD_DIM)
    key_heads = key_row.reshape(seq_len, head_count, HEAD_DIM)
    value_heads = value_row.reshape(seq_len, head_count, HEAD_DIM)
    grad_heads = grad_row.reshape(seq_len, head_count, HEAD_DIM)
    key_grad = jnp.zeros((seq_len, head_count, HEAD_DIM), jnp.float32)
    value_grad = jnp.zeros((seq_len, head_count, HEAD_DIM), jnp.float32)
    query_parts = []
    for offset in range(0, seq_len, block_len):
        query_block = query_heads[offset : offset + block_len]
        grad_block = grad_heads[offset : offset + block_len]
        scores = block_scores(
            query_block, key_heads, seg_row[offset : offset + block_len], seg_row, score_scale
        )
        weights = jnp.exp(scores - log_total[:, offset : offset + block_len, None])
        weights_low = weights.astype(jnp.bfloat16)
        grad_weights = jnp.einsum(
            "qhd,khd->hqk", grad_block, value_heads, preferred_element_type=jnp.float32
        )
        grad_scores = (
            weights * (grad_weights - jnp.sum(weights * grad_weights, axis=-1, keepdims=True))
        ).astype(jnp.bfloat16)
        query_parts.append(
            (
                jnp.einsum(
                    "hqk,khd->qhd", grad_scores, key_heads, preferred_element_type=jnp.float32
                )
                * score_scale
            ).reshape(block_len, head_count * HEAD_DIM)
        )
        key_grad = (
            key_grad
            + jnp.einsum(
                "hqk,qhd->khd", grad_scores, query_block, preferred_element_type=jnp.float32
            )
            * score_scale
        )
        value_grad = value_grad + jnp.einsum(
            "hqk,qhd->khd", weights_low, grad_block, preferred_element_type=jnp.float32
        )
    query_grad = jnp.concatenate(query_parts, axis=0).astype(jnp.bfloat16)
    flat_width = head_count * HEAD_DIM
    return (
        query_grad,
        key_grad.reshape(seq_len, flat_width).astype(jnp.bfloat16),
        value_grad.reshape(seq_len, flat_width).astype(jnp.bfloat16),
    )


def shards(
    inputs,
    segments,
    cotangent,
    norm1_gain,
    norm1_bias,
    qkv_weight,
    qv_bias,
    proj_weight,
    proj_bias,
    norm2_gain,
    norm2_bias,
    fc1_weight,
    fc1_bias,
    fc2_weight,
    fc2_bias,
):
    pack_count, seq_len, model_width = inputs.shape
    row_count = pack_count * seq_len
    local_width = qkv_weight.shape[2]
    row_shape = (pack_count, seq_len, local_width)
    live_rows = (segments > 0).astype(jnp.float32).reshape(row_count, 1)
    flat_in = inputs.reshape(row_count, model_width).astype(jnp.float32)
    norm1_out, norm1_hat, norm1_inv = layer_norm(flat_in, norm1_gain, norm1_bias)
    norm1_low = norm1_out.astype(jnp.bfloat16)
    queries = (product(norm1_low, qkv_weight[0]) + qv_bias[0]).astype(jnp.bfloat16)
    key_rows = product(norm1_low, qkv_weight[1]).astype(jnp.bfloat16)
    value_rows = (product(norm1_low, qkv_weight[2]) + qv_bias[1]).astype(jnp.bfloat16)
    query_packs = queries.reshape(row_shape)
    key_packs = key_rows.reshape(row_shape)
    value_packs = value_rows.reshape(row_shape)
    mixed_rows, log_total = lax.map(row_forward, (query_packs, key_packs, value_packs, segments))
    attended = (mixed_rows.reshape(row_count, local_width) * live_rows).astype(jnp.bfloat16)
    branch = pair_sum(product(attended, proj_weight)) + proj_bias
    middle = flat_in + branch
    norm2_out, norm2_hat, norm2_inv = layer_norm(middle, norm2_gain, norm2_bias)
    norm2_low = norm2_out.astype(jnp.bfloat16)
    hidden = product(norm2_low, fc1_weight) + fc1_bias
    active, gelu_pull = jax.vjp(partial(jax.nn.gelu, approximate=False), hidden)
    active_low = active.astype(jnp.bfloat16)
    result = middle + (pair_sum(product(active_low, fc2_weight)) + fc2_bias)
    output = result.astype(jnp.bfloat16).reshape(pack_count, seq_len, model_width)
    grad_top = cotangent.reshape(row_count, model_width).astype(jnp.float32) * live_rows
    grad_top_low = grad_top.astype(jnp.bfloat16)
    fc2_grad = row_contract(grad_top_low, active_low)
    fc2_bias_grad = jnp.sum(grad_top, axis=0)
    grad_active = back_product(grad_top_low, fc2_weight)
    grad_hidden = gelu_pull(grad_active)[0].astype(jnp.bfloat16)
    fc1_grad = row_contract(norm2_low, grad_hidden)
    fc1_bias_grad = jnp.sum(grad_hidden, axis=0, dtype=jnp.float32)
    grad_norm2 = pair_sum(back_product(grad_hidden, fc1_weight))
    grad_mid_norm, norm2_gain_grad, norm2_bias_grad = norm_back(
        grad_norm2, norm2_hat, norm2_inv, norm2_gain
    )
    grad_middle = grad_top + grad_mid_norm
    grad_branch = grad_middle.astype(jnp.bfloat16)
    proj_grad = row_contract(grad_branch, attended)
    proj_bias_grad = jnp.sum(grad_branch, axis=0, dtype=jnp.float32)
    grad_attended = back_product(grad_branch, proj_weight).astype(jnp.bfloat16) * live_rows.astype(
        jnp.bfloat16
    )
    query_grad, key_grad, value_grad = lax.map(
        row_backward,
        (
            query_packs,
            key_packs,
            value_packs,
            segments,
            grad_attended.reshape(row_shape),
            log_total,
        ),
    )
    query_grad = query_grad.reshape(row_count, local_width)
    key_grad = key_grad.reshape(row_count, local_width)
    value_grad = value_grad.reshape(row_count, local_width)
    qkv_grad = jnp.stack(
        [
            row_contract(norm1_low, query_grad),
            row_contract(norm1_low, key_grad),
            row_contract(norm1_low, value_grad),
        ]
    )
    qv_bias_grad = jnp.stack(
        [
            jnp.sum(query_grad, axis=0, dtype=jnp.float32),
            jnp.sum(value_grad, axis=0, dtype=jnp.float32),
        ]
    )
    grad_norm1 = pair_sum(
        back_product(query_grad, qkv_weight[0])
        + back_product(key_grad, qkv_weight[1])
        + back_product(value_grad, qkv_weight[2])
    )
    grad_in_norm, norm1_gain_grad, norm1_bias_grad = norm_back(
        grad_norm1, norm1_hat, norm1_inv, norm1_gain
    )
    input_grad = (
        (grad_middle + grad_in_norm).astype(jnp.bfloat16).reshape(pack_count, seq_len, model_width)
    )
    qkv_rows = jnp.concatenate([qkv_grad[0], qkv_grad[1], qkv_grad[2]], axis=1)
    block_count = lax.axis_size("dp")
    small_parts = (
        norm1_gain_grad,
        norm1_bias_grad,
        qv_bias_grad[0],
        qv_bias_grad[1],
        proj_bias_grad,
        norm2_gain_grad,
        norm2_bias_grad,
        fc1_bias_grad,
        fc2_bias_grad,
    )
    small_rows = jnp.concatenate([part.reshape(block_count, -1) for part in small_parts], axis=1)
    small_sum = sum_rows(small_rows[:, None, :], Y_FIRST)[0]
    small_out = []
    start = 0
    for part in small_parts:
        width = part.shape[0] // block_count
        small_out.append(small_sum[start : start + width])
        start = start + width
    fc2_sum = sum_rows(blocks_of(fc2_grad, block_count), X_FIRST).T
    fc1_sum = sum_rows(blocks_of(fc1_grad, block_count), Y_FIRST)
    proj_sum = sum_rows(blocks_of(proj_grad, block_count), Z_FIRST).T
    qkv_sum = sum_rows(blocks_of(qkv_rows, block_count), X_FIRST)
    qkv_sum = jnp.stack(jnp.split(qkv_sum, 3, axis=1))
    return (
        output,
        input_grad,
        small_out[0],
        small_out[1],
        qkv_sum,
        jnp.stack([small_out[2], small_out[3]]),
        proj_sum,
        small_out[4],
        small_out[5],
        small_out[6],
        fc1_sum,
        small_out[7],
        fc2_sum,
        small_out[8],
    )


def solution(mesh):
    placed = (
        P("dp", None, None),
        P("dp", None),
        P("dp", None, None),
        P(),
        P(),
        P(None, None, "mp"),
        P(None, "mp"),
        P("mp", None),
        P(),
        P(),
        P(),
        P(None, "mp"),
        P("mp"),
        P("mp", None),
        P(),
    )
    return jax.shard_map(
        shards,
        mesh=mesh,
        in_specs=placed,
        out_specs=(
            P("dp", None, None),
            P("dp", None, None),
            P("dp"),
            P("dp"),
            P(None, "dp", "mp"),
            P(None, ("mp", "dp")),
            P("mp", "dp"),
            P("dp"),
            P("dp"),
            P("dp"),
            P("dp", "mp"),
            P(("mp", "dp")),
            P("mp", "dp"),
            P("dp"),
        ),
        check_vma=False,
    )
```
